32 devices in a mesh: dp: 8 (over z, x), tensor: 4 (over y, core).
Axes of the slice: x: 2, y: 2, z: 4, core: 2. Of those that a mesh axis runs over, the one named last changes fastest.
Arguments:
- tokens: bfloat16 [4096, 1024], P(('dp', 'tensor')), may hold values from -6 to 6
- cotangent: bfloat16 [4096, 1024], P(('dp', 'tensor')), may hold values from -6 to 6
- norm1_gain: bfloat16 [1024], P('dp'), may hold values from 0.5 to 1.5
- w_query: bfloat16 [1024, 1024], P('dp', 'tensor'), may hold values from -0.1875 to 0.1875
- w_key: bfloat16 [1024, 1024], P('dp', 'tensor'), may hold values from -0.1875 to 0.1875
- w_value: bfloat16 [1024, 2048], P('dp', 'tensor'), may hold values from -0.1875 to 0.1875
- w_gate_out: bfloat16 [1024, 2048], P('dp', 'tensor'), may hold values from -0.1875 to 0.1875
- w_out: bfloat16 [1024, 2048], P('dp', 'tensor'), may hold values from -0.1875 to 0.1875
- w_beta: bfloat16 [1024, 8], P('dp', 'tensor'), may hold values from -0.1875 to 0.1875
- w_alpha: bfloat16 [1024, 8], P('dp', 'tensor'), may hold values from -0.1875 to 0.1875
- conv_query: bfloat16 [128, 8, 4], P('dp', 'tensor'), may hold values from -3 to 3
- conv_key: bfloat16 [128, 8, 4], P('dp', 'tensor'), may hold values from -3 to 3
- conv_value: bfloat16 [256, 8, 4], P('dp', 'tensor'), may hold values from -3 to 3
- a_log: bfloat16 [8], P('tensor'), may hold values from 0 to 2.765625
- dt_bias: bfloat16 [8], P('tensor'), may hold values from -6.875 to -2.296875
- head_gain: bfloat16 [256, 8], P('dp', 'tensor'), may hold values from 0.5 to 1.5
- norm2_gain: bfloat16 [1024], P('dp'), may hold values from 0.5 to 1.5
- w_up_gate: bfloat16 [1024, 2816], P('dp', 'tensor'), may hold values from -0.1875 to 0.1875
- w_up: bfloat16 [1024, 2816], P('dp', 'tensor'), may hold values from -0.1875 to 0.1875
- w_down: bfloat16 [1024, 2816], P('dp', 'tensor'), may hold values from -0.109375 to 0.109375
Outputs:
- out: bfloat16 [4096, 1024], P(('dp', 'tensor'))
- grad_tokens: float32 [4096, 1024], P(('dp', 'tensor'))
- grad_norm1_gain: float32 [1024], P('dp')
- grad_w_query: float32 [1024, 1024], P('dp', 'tensor')
- grad_w_key: float32 [1024, 1024], P('dp', 'tensor')
- grad_w_value: float32 [1024, 2048], P('dp', 'tensor')
- grad_w_gate_out: float32 [1024, 2048], P('dp', 'tensor')
- grad_w_out: float32 [1024, 2048], P('dp', 'tensor')
- grad_w_beta: float32 [1024, 8], P('dp', 'tensor')
- grad_w_alpha: float32 [1024, 8], P('dp', 'tensor')
- grad_conv_query: float32 [128, 8, 4], P('dp', 'tensor')
- grad_conv_key: float32 [128, 8, 4], P('dp', 'tensor')
- grad_conv_value: float32 [256, 8, 4], P('dp', 'tensor')
- grad_a_log: float32 [8], P('tensor')
- grad_dt_bias: float32 [8], P('tensor')
- grad_head_gain: float32 [256, 8], P('dp', 'tensor')
- grad_norm2_gain: float32 [1024], P('dp')
- grad_w_up_gate: float32 [1024, 2816], P('dp', 'tensor')
- grad_w_up: float32 [1024, 2816], P('dp', 'tensor')
- grad_w_down: float32 [1024, 2816], P('dp', 'tensor')
The draws below stay inside these ranges and needn't reach their ends.
All inputs are finite; a program needn't handle non-finite values.
Results may differ from the reference program's by a relative error of at most 0.012.
Values may be sent and summed in bfloat16 or wider, within the bound.
A program may use at most 128 MiB of HBM per device.

```python
from functools import partial
import jax
import jax.numpy as jnp
from jax import lax

D = 1024
H = 8
DK = 128
DV = 256
FF = 2816
CONV = 4
BLOCK = 64
SEQ = 512
TOKENS = 4096


def level_of(own_key, dims, cuts, smallest, high):
    factor_of = 1.0
    for dim, parts in cuts:
        draws = jax.random.uniform(jax.random.fold_in(jax.random.fold_in(own_key, 6), dim), (parts,), jnp.float32, smallest / len(cuts), high / len(cuts))
        factor_of = factor_of * jnp.repeat(jnp.exp(draws), dims[dim] // parts).reshape((-1,) + (1,) * (len(dims) - 1 - dim))
    return factor_of


def centred(key, extent, width, most, cuts=(), kind=jnp.bfloat16):
    factor_of = level_of(key, extent, cuts, -0.22, 0.18) if cuts else 1.0
    drawn = jax.random.normal(key, extent, jnp.float32) * width * factor_of
    return jnp.minimum(jnp.maximum(drawn, -most), most).astype(kind)


def setup_inputs(seed: int = 0) -> dict:
    splits = jax.random.split(jax.random.key(seed), 21)
    tokens = centred(splits[0], (TOKENS, D), 1.0, 6.0, ((0, 32),))
    cotangent = centred(splits[1], (TOKENS, D), 1.0, 6.0, ((0, 32),))
    norm1_gain = jnp.clip(1.0 + 0.1 * jax.random.normal(splits[2], (D,), jnp.float32), 0.5, 1.5).astype(jnp.bfloat16)
    w_query = centred(splits[3], (D, H * DK), D ** -0.5, 0.1875, ((0, 8), (1, 4)))
    w_key = centred(splits[4], (D, H * DK), D ** -0.5, 0.1875, ((0, 8), (1, 4)))
    w_value = centred(splits[5], (D, H * DV), D ** -0.5, 0.1875, ((0, 8), (1, 4)))
    w_gate_out = centred(splits[6], (D, H * DV), D ** -0.5, 0.1875, ((0, 8), (1, 4)))
    w_out = centred(splits[7], (D, H * DV), (H * DV // 2) ** -0.5, 0.1875, ((0, 8), (1, 4)))
    w_beta = centred(splits[8], (D, H), D ** -0.5, 0.1875, ((0, 8), (1, 4)))
    w_alpha = centred(splits[9], (D, H), D ** -0.5, 0.1875, ((0, 8), (1, 4)))
    conv_query = centred(splits[10], (DK, H, CONV), CONV ** -0.5, 3.0, ((0, 8), (1, 4)))
    conv_key = centred(splits[11], (DK, H, CONV), CONV ** -0.5, 3.0, ((0, 8), (1, 4)))
    conv_value = centred(splits[12], (DV, H, CONV), CONV ** -0.5, 3.0, ((0, 8), (1, 4)))
    a_log = jnp.clip(2.765625 * jax.random.uniform(splits[13], (H,), jnp.float32) ** level_of(splits[13], (H,), ((0, 4),), -0.2, 0.2), 0.0, 2.765625).astype(jnp.bfloat16)
    dt_bias = jnp.clip(-6.875 + 4.578125 * jax.random.uniform(splits[14], (H,), jnp.float32) ** level_of(splits[14], (H,), ((0, 4),), -0.2, 0.2), -6.875, -2.296875).astype(jnp.bfloat16)
    head_gain = jnp.clip(1.0 + 0.1 * jax.random.normal(splits[15], (DV, H), jnp.float32), 0.5, 1.5).astype(jnp.bfloat16)
    norm2_gain = jnp.clip(1.0 + 0.1 * jax.random.normal(splits[16], (D,), jnp.float32), 0.5, 1.5).astype(jnp.bfloat16)
    w_up_gate = centred(splits[17], (D, FF), D ** -0.5, 0.1875, ((0, 8), (1, 4)))
    w_up = centred(splits[18], (D, FF), D ** -0.5, 0.1875, ((0, 8), (1, 4)))
    w_down = centred(splits[19], (D, FF), FF ** -0.5, 0.109375, ((0, 8), (1, 4)))
    return {"tokens": tokens, "cotangent": cotangent, "norm1_gain": norm1_gain, "w_query": w_query, "w_key": w_key, "w_value": w_value, "w_gate_out": w_gate_out, "w_out": w_out, "w_beta": w_beta, "w_alpha": w_alpha, "conv_query": conv_query, "conv_key": conv_key, "conv_value": conv_value, "a_log": a_log, "dt_bias": dt_bias, "head_gain": head_gain, "norm2_gain": norm2_gain, "w_up_gate": w_up_gate, "w_up": w_up, "w_down": w_down}


epsilon = 1e-06
highest = lax.Precision.HIGHEST
contract_rows = (((0,), (0,)), ((), ()))
contract_cols = (((1,), (1,)), ((), ()))

def norm_forward(row_values):
    row_scale = lax.rsqrt(lax.optimization_barrier(jnp.mean(row_values * row_values, axis=-1, keepdims=True)) + epsilon)
    return (row_scale, row_values * row_scale)

def norm_backward(grad_normed, unit_values, row_scale, gain_values):
    grad_unit = grad_normed * gain_values
    return row_scale * (grad_unit - unit_values * lax.optimization_barrier(jnp.mean(grad_unit * unit_values, axis=-1, keepdims=True)))

def short_conv(inputs, weights):
    tap_count = weights.shape[1]
    row_count = inputs.shape[0]
    padded = jnp.pad(inputs, ((tap_count - 1, 0), (0, 0)))
    result = jnp.zeros_like(inputs)
    for offset in range(tap_count):
        result = result + padded[offset:offset + row_count] * weights[:, offset]
    return result

def unit_length(values):
    return values * lax.rsqrt(lax.optimization_barrier(jnp.sum(values * values, axis=-1, keepdims=True)) + epsilon)

def split_heads(matrix_in, head_count):
    row_count, total_width = matrix_in.shape
    return jnp.swapaxes(matrix_in.reshape(row_count, head_count, total_width // head_count), 0, 1)

def channel_weights(conv_weights):
    key_dim, head_count, tap_count = conv_weights.shape
    return jnp.swapaxes(conv_weights, 0, 1).reshape(head_count * key_dim, tap_count)

def delta_rule(queries, keys_in, values, beta_rows, log_gates):
    head_count, seq_rows, key_dim = queries.shape
    value_dim = values.shape[2]
    block_count = seq_rows // BLOCK

    def blocked(matrix_in):
        return jnp.swapaxes(matrix_in.reshape((head_count, block_count, BLOCK) + matrix_in.shape[2:]), 0, 1)
    lower_incl = jnp.tril(jnp.ones((BLOCK, BLOCK), dtype=bool))
    lower_strict = jnp.tril(jnp.ones((BLOCK, BLOCK), dtype=bool), -1)
    identity_mat = jnp.eye(BLOCK, dtype=jnp.float32)
    solver = jax.vmap(partial(jax.scipy.linalg.solve_triangular, lower=True, unit_diagonal=True))

    def advance(carry_state, pieces):
        query_blk, key_blk, value_blk, beta_blk, gate_blk = pieces
        cum_decay = jnp.cumsum(gate_blk, axis=-1)
        differ = cum_decay[:, :, None] - cum_decay[:, None, :]
        decay_mat = jnp.where(lower_incl, jnp.exp(jnp.where(lower_incl, differ, 0.0)), 0.0)
        key_gram = jnp.einsum('hid,hjd->hij', key_blk, key_blk, precision=highest)
        system = identity_mat + jnp.where(lower_strict, key_gram * decay_mat * beta_blk[:, :, None], 0.0)
        right_side = jnp.concatenate([key_blk * (beta_blk * jnp.exp(cum_decay))[:, :, None], value_blk * beta_blk[:, :, None]], axis=-1)
        solved = solver(system, right_side)
        key_part = solved[..., :key_dim]
        value_part = solved[..., key_dim:]
        fresh_values = value_part - jnp.einsum('hcd,hde->hce', key_part, carry_state, precision=highest)
        scores = jnp.einsum('hid,hjd->hij', query_blk, key_blk, precision=highest) * decay_mat
        output_blk = jnp.einsum('hcd,hde->hce', query_blk * jnp.exp(cum_decay)[:, :, None], carry_state, precision=highest)
        output_blk = output_blk + jnp.einsum('hij,hje->hie', scores, fresh_values, precision=highest)
        final_decay = cum_decay[:, -1]
        carried = jnp.exp(final_decay)[:, None, None] * carry_state
        carry_state = carried + jnp.einsum('hcd,hce->hde', key_blk * jnp.exp(final_decay[:, None] - cum_decay)[:, :, None], fresh_values, precision=highest)
        return (carry_state, output_blk)
    initial = jnp.zeros((head_count, key_dim, value_dim), jnp.float32)
    unused, outputs = lax.scan(advance, initial, (blocked(queries), blocked(keys_in), blocked(values), blocked(beta_rows), blocked(log_gates)))
    return jnp.swapaxes(outputs, 0, 1).reshape(head_count, seq_rows, value_dim)

def mixer_piece(proj_query, proj_key, proj_value, proj_gate, proj_beta, proj_alpha, conv_q_w, conv_k_w, conv_v_w, gain_heads, log_rate, rate_bias):
    head_count = proj_beta.shape[1]
    queries = split_heads(jax.nn.silu(short_conv(proj_query, channel_weights(conv_q_w))), head_count)
    queries = unit_length(queries) * queries.shape[2] ** (-0.5)
    keys_in = unit_length(split_heads(jax.nn.silu(short_conv(proj_key, channel_weights(conv_k_w))), head_count))
    values = split_heads(jax.nn.silu(short_conv(proj_value, channel_weights(conv_v_w))), head_count)
    beta_rows = jax.nn.sigmoid(proj_beta).T
    log_gates = -jnp.exp(log_rate)[:, None] * jax.nn.softplus(proj_alpha + rate_bias).T
    mixed = delta_rule(queries, keys_in, values, beta_rows, log_gates)
    scaled = mixed * lax.rsqrt(lax.optimization_barrier(jnp.mean(mixed * mixed, axis=-1, keepdims=True)) + epsilon) * gain_heads.T[:, None, :]
    gated = scaled * split_heads(jax.nn.silu(proj_gate), head_count)
    return jnp.swapaxes(gated, 0, 1).reshape(gated.shape[1], -1)

def weight_grad(left_in, right_in):
    return lax.dot_general(left_in.astype(jnp.float32), right_in.astype(jnp.float32), contract_rows, preferred_element_type=jnp.float32)

def times_transpose(left_in, right_in):
    return lax.dot_general(left_in.astype(jnp.float32), right_in.astype(jnp.float32), contract_cols, preferred_element_type=jnp.float32)

def reference(tokens, cotangent, norm1_gain, w_query, w_key, w_value, w_gate_out, w_out, w_beta, w_alpha, conv_query, conv_key, conv_value, a_log, dt_bias, head_gain, norm2_gain, w_up_gate, w_up, w_down):
    small_params = tuple((param.astype(jnp.float32) for param in (conv_query, conv_key, conv_value, head_gain, a_log, dt_bias)))
    gain_one = norm1_gain.astype(jnp.float32)
    gain_two = norm2_gain.astype(jnp.float32)
    mixer_mats = (w_query, w_key, w_value, w_gate_out, w_beta, w_alpha)
    grad_params = (norm1_gain, w_query, w_key, w_value, w_gate_out, w_out, w_beta, w_alpha, conv_query, conv_key, conv_value, a_log, dt_bias, head_gain, norm2_gain, w_up_gate, w_up, w_down)

    def one_sequence(totals, paired):
        seq_tokens, seq_cot = paired
        row_values = seq_tokens.astype(jnp.float32)
        scale_one, unit_one = norm_forward(row_values)
        normed_one = (unit_one * gain_one).astype(jnp.bfloat16)
        projected = [jnp.dot(normed_one.astype(jnp.float32), weight.astype(jnp.float32), preferred_element_type=jnp.float32) for weight in mixer_mats]
        mixed_full, pullback = jax.vjp(mixer_piece, *projected, *small_params)
        mixed = mixed_full.astype(jnp.bfloat16)
        middle = row_values + times_transpose(mixed, w_out)
        scale_two, unit_two = norm_forward(middle)
        normed_two = (unit_two * gain_two).astype(jnp.bfloat16)
        up_gate = jnp.dot(normed_two.astype(jnp.float32), w_up_gate.astype(jnp.float32), preferred_element_type=jnp.float32)
        up_lin = jnp.dot(normed_two.astype(jnp.float32), w_up.astype(jnp.float32), preferred_element_type=jnp.float32)
        hidden = (jax.nn.silu(up_gate) * up_lin).astype(jnp.bfloat16)
        result = (middle + times_transpose(hidden, w_down)).astype(jnp.bfloat16)
        grad_hidden = jnp.dot(seq_cot.astype(jnp.float32), w_down.astype(jnp.float32), preferred_element_type=jnp.float32)
        grad_down = weight_grad(seq_cot, hidden)
        gate_sigmoid = jax.nn.sigmoid(up_gate)
        grad_gate = (grad_hidden * up_lin * gate_sigmoid * (1.0 + up_gate * (1.0 - gate_sigmoid))).astype(jnp.bfloat16)
        grad_lin = (grad_hidden * up_gate * gate_sigmoid).astype(jnp.bfloat16)
        grad_up_gate = weight_grad(normed_two, grad_gate)
        grad_up = weight_grad(normed_two, grad_lin)
        grad_normed_two = times_transpose(grad_gate, w_up_gate) + times_transpose(grad_lin, w_up)
        grad_gain_two = lax.optimization_barrier(jnp.sum(grad_normed_two * unit_two, axis=0))
        grad_middle = seq_cot.astype(jnp.float32) + norm_backward(grad_normed_two, unit_two, scale_two, gain_two)
        grad_mid = grad_middle.astype(jnp.bfloat16)
        grad_out_w = weight_grad(grad_mid, mixed)
        grad_mixed = jnp.dot(grad_mid.astype(jnp.float32), w_out.astype(jnp.float32), preferred_element_type=jnp.float32)
        pulled = pullback(grad_mixed)
        grad_proj = [grad_piece.astype(jnp.bfloat16) for grad_piece in pulled[:6]]
        grad_mats = [weight_grad(normed_one, grad_piece) for grad_piece in grad_proj]
        grad_normed_one = sum((times_transpose(grad_piece, weight) for grad_piece, weight in zip(grad_proj, mixer_mats)))
        grad_gain_one = lax.optimization_barrier(jnp.sum(grad_normed_one * unit_one, axis=0))
        grad_rows = grad_middle + norm_backward(grad_normed_one, unit_one, scale_one, gain_one)
        grads = (grad_gain_one, grad_mats[0], grad_mats[1], grad_mats[2], grad_mats[3], grad_out_w, grad_mats[4], grad_mats[5], pulled[6], pulled[7], pulled[8], pulled[10], pulled[11], pulled[9], grad_gain_two, grad_up_gate, grad_up, grad_down)
        totals = tuple((total + grad_piece for total, grad_piece in zip(totals, grads)))
        return (totals, (result, grad_rows))
    initial = tuple((jnp.zeros(param.shape, jnp.float32) for param in grad_params))
    seq_tokens_all = tokens.reshape(-1, SEQ, D)
    seq_cot_all = cotangent.reshape(-1, SEQ, D)
    totals, stacked = lax.scan(one_sequence, initial, (seq_tokens_all, seq_cot_all))
    result_all = stacked[0].reshape(-1, D)
    grad_all = stacked[1].reshape(-1, D)
    return (result_all, grad_all, totals[0], totals[1], totals[2], totals[3], totals[4], totals[5], totals[6], totals[7], totals[8], totals[9], totals[10], totals[11], totals[12], totals[13], totals[14], totals[15], totals[16], totals[17])
```

```python
import jax
import jax.numpy as jnp
from jax import lax
from jax.experimental import pallas as pl
from jax.experimental.pallas import tpu as pltpu
from jax.sharding import PartitionSpec as P

epsilon = 1e-06
CHUNK = 128
LANES = 128
contract_rows = (((0,), (0,)), ((), ()))
contract_cols = (((1,), (1,)), ((), ()))
contract_plain = (((1,), (0,)), ((), ()))
highest = lax.Precision.HIGHEST


def norm_forward(row_values):
    row_scale = lax.rsqrt(jnp.mean(row_values * row_values, axis=-1, keepdims=True) + epsilon)
    return (row_scale, row_values * row_scale)


def norm_backward(grad_normed, unit_values, row_scale, gain_values):
    grad_unit = grad_normed * gain_values
    return row_scale * (
        grad_unit - unit_values * jnp.mean(grad_unit * unit_values, axis=-1, keepdims=True)
    )


def weight_grad(left_in, right_in):
    return lax.dot_general(left_in, right_in, contract_rows, preferred_element_type=jnp.float32)


def times_transpose(left_in, right_in):
    return lax.dot_general(left_in, right_in, contract_cols, preferred_element_type=jnp.float32)


def exact_dot(left_in, right_in, dims=contract_plain):
    return lax.dot_general(
        left_in, right_in, dims, precision=highest, preferred_element_type=jnp.float32
    )


def silu(values):
    return values * lax.logistic(values)


def unit_length(values):
    return values * lax.rsqrt(jnp.sum(values * values, axis=-1, keepdims=True) + epsilon)


def triangle_masks(size):
    row = lax.broadcasted_iota(jnp.int32, (size, size), 0)
    col = lax.broadcasted_iota(jnp.int32, (size, size), 1)
    return row, col


def unit_lower_inverse(lower):
    size = lower.shape[0]
    row, col = triangle_masks(size)
    inverse = jnp.where(row == col, 1.0, 0.0)
    bit = 0
    while (1 << bit) < size:
        joined = ((row >> (bit + 1)) == (col >> (bit + 1))) & ((row >> bit) != (col >> bit))
        part = jnp.where(joined, lower, 0.0)
        if bit == 0:
            inverse = inverse - part
        else:
            inverse = inverse - exact_dot(inverse, exact_dot(part, inverse))
        bit += 1
    return inverse


@jax.custom_vjp
def known_inverse(lower, inverse):
    return inverse


def known_inverse_fwd(lower, inverse):
    return inverse, inverse


def known_inverse_bwd(inverse, grad):
    turned = inverse.T
    return -exact_dot(exact_dot(turned, grad), turned), jnp.zeros_like(inverse)


known_inverse.defvjp(known_inverse_fwd, known_inverse_bwd)


def mixer_chunk(conv_q, conv_k, conv_v, proj_gate, beta, gate, gain, state, inverter):
    size, key_dim = conv_q.shape
    row, col = triangle_masks(size)
    strict = row > col
    lower = row >= col
    query = unit_length(silu(conv_q)) * key_dim ** (-0.5)
    key = unit_length(silu(conv_k))
    value = silu(conv_v)
    wide = jnp.broadcast_to(gate, (size, size))
    decay_col = jnp.sum(jnp.where(lower, wide.T, 0.0), axis=1, keepdims=True)
    decay_row = jnp.sum(jnp.where(row <= col, wide, 0.0), axis=0, keepdims=True)
    decay_end = jnp.sum(gate, axis=0, keepdims=True)
    differ = jnp.where(strict, decay_col - decay_row, 0.0)
    decay = jnp.where(lower, jnp.exp(differ), 0.0)
    system = jnp.where(strict, exact_dot(key, key, contract_cols) * decay * beta, 0.0)
    inverse = inverter(system)
    grown = jnp.exp(decay_col)
    fresh = exact_dot(inverse, value * beta - exact_dot(key * (beta * grown), state))
    scores = exact_dot(query, key, contract_cols) * decay
    mixed = exact_dot(query * grown, state) + exact_dot(scores, fresh)
    new_state = jnp.exp(decay_end) * state + exact_dot(
        key * jnp.exp(decay_end - decay_col), fresh, contract_rows
    )
    scaled = mixed * lax.rsqrt(jnp.mean(mixed * mixed, axis=-1, keepdims=True) + epsilon) * gain
    return scaled * silu(proj_gate), new_state, inverse


def head_slices(head, heads, key_dim, value_dim):
    q_at = head * key_dim
    k_at = (heads + head) * key_dim
    v_at = 2 * heads * key_dim + head * value_dim
    return (
        slice(q_at, q_at + key_dim),
        slice(k_at, k_at + key_dim),
        slice(v_at, v_at + value_dim),
        slice(head * value_dim, (head + 1) * value_dim),
    )


def mixer_forward_kernel(
    heads, key_dim, value_dim, conv_ref, pgate_ref, rates_ref, gain_ref,
    gated_ref, states_ref, inverses_ref, state_ref,
):
    @pl.when(pl.program_id(0) == 0)
    def _():
        state_ref[...] = jnp.zeros_like(state_ref)

    for head in range(heads):
        at_q, at_k, at_v, at_g = head_slices(head, heads, key_dim, value_dim)
        state = state_ref[head]
        gated, new_state, inverse = mixer_chunk(
            conv_ref[:, at_q],
            conv_ref[:, at_k],
            conv_ref[:, at_v],
            pgate_ref[:, at_g],
            rates_ref[:, head : head + 1],
            rates_ref[:, heads + head : heads + head + 1],
            gain_ref[:, at_g],
            state,
            unit_lower_inverse,
        )
        gated_ref[:, at_g] = gated.astype(gated_ref.dtype)
        states_ref[0, head] = state
        inverses_ref[0, head] = inverse
        state_ref[head] = new_state


def mixer_backward_kernel(
    heads, key_dim, value_dim, conv_ref, pgate_ref, rates_ref, gain_ref, states_ref,
    inverses_ref, grad_ref, gconv_ref, gpgate_ref, grates_ref, ggain_ref, gstate_ref,
):
    @pl.when(pl.program_id(0) == 0)
    def _():
        gstate_ref[...] = jnp.zeros_like(gstate_ref)
        ggain_ref[...] = jnp.zeros_like(ggain_ref)

    lane = lax.broadcasted_iota(jnp.int32, grates_ref.shape, 1)
    rates_grad = jnp.zeros(grates_ref.shape, jnp.float32)
    for head in range(heads):
        at_q, at_k, at_v, at_g = head_slices(head, heads, key_dim, value_dim)
        inverse = inverses_ref[0, head]

        def run(*operands):
            gated, new_state, _ = mixer_chunk(
                *operands, lambda system: known_inverse(system, inverse)
            )
            return gated, new_state

        _, pull = jax.vjp(
            run,
            conv_ref[:, at_q],
            conv_ref[:, at_k],
            conv_ref[:, at_v],
            pgate_ref[:, at_g],
            rates_ref[:, head : head + 1],
            rates_ref[:, heads + head : heads + head + 1],
            gain_ref[:, at_g],
            states_ref[0, head],
        )
        pulled = pull((grad_ref[:, at_g], gstate_ref[head]))
        gconv_ref[:, at_q] = pulled[0]
        gconv_ref[:, at_k] = pulled[1]
        gconv_ref[:, at_v] = pulled[2]
        gpgate_ref[:, at_g] = pulled[3]
        rates_grad = jnp.where(lane == head, pulled[4], rates_grad)
        rates_grad = jnp.where(lane == heads + head, pulled[5], rates_grad)
        ggain_ref[:, at_g] += pulled[6]
        gstate_ref[head] = pulled[7]
    grates_ref[...] = rates_grad


def row_block(width, order):
    return pl.BlockSpec((CHUNK, width), lambda step: (order(step), 0))


def mixer_forward(conv_all, proj_gate, rates, gain_row, heads, key_dim, value_dim):
    rows, conv_width = conv_all.shape
    steps = rows // CHUNK
    forward = lambda step: step
    width = heads * value_dim
    return pl.pallas_call(
        lambda *refs: mixer_forward_kernel(heads, key_dim, value_dim, *refs),
        name="mixer_forward",
        grid=(steps,),
        in_specs=[
            row_block(conv_width, forward),
            row_block(width, forward),
            row_block(rates.shape[1], forward),
            pl.BlockSpec((1, width), lambda step: (0, 0)),
        ],
        out_specs=[
            row_block(width, forward),
            pl.BlockSpec((1, heads, key_dim, value_dim), lambda step: (step, 0, 0, 0)),
            pl.BlockSpec((1, heads, CHUNK, CHUNK), lambda step: (step, 0, 0, 0)),
        ],
        out_shape=[
            jax.ShapeDtypeStruct((rows, width), jnp.bfloat16),
            jax.ShapeDtypeStruct((steps, heads, key_dim, value_dim), jnp.float32),
            jax.ShapeDtypeStruct((steps, heads, CHUNK, CHUNK), jnp.float32),
        ],
        scratch_shapes=[pltpu.VMEM((heads, key_dim, value_dim), jnp.float32)],
        cost_estimate=pl.CostEstimate(
            flops=80_000_000_00, bytes_accessed=8_000_000, transcendentals=1_000_000
        ),
    )(conv_all, proj_gate, rates, gain_row)


def mixer_backward(
    conv_all, proj_gate, rates, gain_row, states, inverses, grad_gated, heads, key_dim, value_dim
):
    rows, conv_width = conv_all.shape
    steps = rows // CHUNK
    back = lambda step: steps - 1 - step
    width = heads * value_dim
    return pl.pallas_call(
        lambda *refs: mixer_backward_kernel(heads, key_dim, value_dim, *refs),
        name="mixer_backward",
        grid=(steps,),
        in_specs=[
            row_block(conv_width, back),
            row_block(width, back),
            row_block(rates.shape[1], back),
            pl.BlockSpec((1, width), lambda step: (0, 0)),
            pl.BlockSpec((1, heads, key_dim, value_dim), lambda step: (back(step), 0, 0, 0)),
            pl.BlockSpec((1, heads, CHUNK, CHUNK), lambda step: (back(step), 0, 0, 0)),
            row_block(width, back),
        ],
        out_specs=[
            row_block(conv_width, back),
            row_block(width, back),
            row_block(rates.shape[1], back),
            pl.BlockSpec((1, width), lambda step: (0, 0)),
        ],
        out_shape=[
            jax.ShapeDtypeStruct((rows, conv_width), jnp.float32),
            jax.ShapeDtypeStruct((rows, width), jnp.float32),
            jax.ShapeDtypeStruct(rates.shape, jnp.float32),
            jax.ShapeDtypeStruct((1, width), jnp.float32),
        ],
        scratch_shapes=[pltpu.VMEM((heads, key_dim, value_dim), jnp.float32)],
        cost_estimate=pl.CostEstimate(
            flops=200_000_000_00, bytes_accessed=12_000_000, transcendentals=2_000_000
        ),
    )(conv_all, proj_gate, rates, gain_row, states, inverses, grad_gated)


def short_conv(inputs, weights):
    tap_count = weights.shape[1]
    row_count = inputs.shape[0]
    padded = jnp.pad(inputs, ((tap_count - 1, 0), (0, 0)))
    result = jnp.zeros_like(inputs)
    for offset in range(tap_count):
        result = result + padded[offset : offset + row_count] * weights[:, offset]
    return result


def channel_weights(conv_weights):
    key_dim, head_count, tap_count = conv_weights.shape
    return jnp.swapaxes(conv_weights, 0, 1).reshape(head_count * key_dim, tap_count)


def pad_columns(matrix_in, width):
    return jnp.pad(matrix_in, ((0, 0), (0, width - matrix_in.shape[1])))


def round_up(size, step):
    return -(-size // step) * step


def as_columns(values, rows):
    flat = values.reshape(-1)
    return jnp.pad(flat, (0, round_up(flat.shape[0], rows) - flat.shape[0])).reshape(rows, -1)


def rate_terms(proj_beta, proj_alpha, log_rate, rate_bias):
    log_gates = -jnp.exp(log_rate) * jax.nn.softplus(proj_alpha + rate_bias)
    return jnp.concatenate([jax.nn.sigmoid(proj_beta), log_gates], axis=1)


def on_device(
    tokens, cotangent, norm1_gain, w_query, w_key, w_value, w_gate_out, w_out, w_beta, w_alpha,
    conv_query, conv_key, conv_value, a_log, dt_bias, head_gain, norm2_gain, w_up_gate, w_up,
    w_down,
):
    bf16, f32 = jnp.bfloat16, jnp.float32
    shard_rows, model = w_query.shape[0], tokens.shape[1]
    dp = model // shard_rows
    heads = a_log.shape[0]
    key_dim, value_dim = w_query.shape[1] // heads, w_value.shape[1] // heads
    taps = conv_query.shape[2]
    qk_width, v_width = heads * key_dim, heads * value_dim
    conv_width = 2 * qk_width + v_width
    hidden_width = w_up.shape[1]
    ff = round_up(hidden_width, 256)

    small_arrays = (norm1_gain, norm2_gain, conv_query, conv_key, conv_value, head_gain)
    small_cols = [as_columns(values, shard_rows) for values in small_arrays]
    counts = [cols.shape[1] for cols in small_cols]
    small = pad_columns(jnp.concatenate([w_beta, w_alpha] + small_cols, axis=1), LANES)
    mixer_pack = jnp.concatenate([w_query, w_key, w_value, w_gate_out, small, w_out], axis=1)
    in_width = conv_width + v_width + LANES
    rows_pack = jnp.concatenate([tokens, cotangent], axis=1)
    rows_full = lax.all_gather(rows_pack, "tensor", axis=0, tiled=True)
    mixer_full = lax.all_gather(mixer_pack, "dp", axis=0, tiled=True)
    ffn_pack = jnp.concatenate([pad_columns(w, ff) for w in (w_up_gate, w_up, w_down)], axis=1)
    mixer_full, ffn_pack = lax.optimization_barrier((mixer_full, ffn_pack))
    ffn_full = lax.all_gather(ffn_pack, "dp", axis=0, tiled=True)

    in_full = mixer_full[:, :in_width]
    out_full = mixer_full[:, in_width:]
    starts = [2 * heads]
    for count in counts:
        starts.append(starts[-1] + count)
    small_at = conv_width + v_width

    def unpacked(index):
        cols = mixer_full[:, small_at + starts[index] : small_at + starts[index + 1]]
        shape = small_arrays[index].shape
        size = small_arrays[index].size
        shards = cols.reshape(dp, -1)[:, :size]
        return shards.reshape((dp * shape[0],) + shape[1:]).astype(f32)

    gain_one, gain_two = unpacked(0), unpacked(1)
    conv_weights = jnp.concatenate([channel_weights(unpacked(i)) for i in (2, 3, 4)], axis=0)
    gain_row = unpacked(5).T.reshape(1, v_width)

    tokens_full = rows_full[:, :model].astype(f32)
    cot_full = rows_full[:, model:]
    _, unit_full = norm_forward(tokens_full)
    normed_one = (unit_full * gain_one).astype(bf16)
    projected = jnp.dot(normed_one, in_full, preferred_element_type=f32)
    proj_conv = projected[:, :conv_width]
    proj_gate = projected[:, conv_width:small_at]
    proj_beta = projected[:, small_at : small_at + heads]
    proj_alpha = projected[:, small_at + heads : small_at + 2 * heads]
    conv_all, conv_pull = jax.vjp(short_conv, proj_conv, conv_weights)
    rates, rates_pull = jax.vjp(
        rate_terms, proj_beta, proj_alpha, a_log.astype(f32), dt_bias.astype(f32)
    )
    mixed, states, inverses = mixer_forward(
        conv_all, proj_gate, rates, gain_row, heads, key_dim, value_dim
    )
    row_values = tokens.astype(f32)
    scale_one, unit_one = norm_forward(row_values)
    middle = row_values + lax.psum_scatter(
        times_transpose(mixed, out_full).astype(bf16), "tensor", scatter_dimension=0, tiled=True
    ).astype(f32)
    gates_full, down_full = ffn_full[:, : 2 * ff], ffn_full[:, 2 * ff :]
    grad_hidden = jnp.dot(cot_full, down_full, preferred_element_type=f32)
    scale_two, unit_two = norm_forward(middle)
    normed_two = lax.all_gather(
        (unit_two * gain_two).astype(bf16), "tensor", axis=0, tiled=True
    )
    ups = jnp.dot(normed_two, gates_full, preferred_element_type=f32)
    up_gate, up_lin = ups[:, :ff], ups[:, ff:]
    gate_sigmoid = jax.nn.sigmoid(up_gate)
    hidden = (up_gate * gate_sigmoid * up_lin).astype(bf16)
    grad_gate = (
        grad_hidden * up_lin * gate_sigmoid * (1.0 + up_gate * (1.0 - gate_sigmoid))
    ).astype(bf16)
    grad_lin = (grad_hidden * up_gate * gate_sigmoid).astype(bf16)
    grad_ups = jnp.concatenate([grad_gate, grad_lin], axis=1)
    grad_normed_two = lax.psum_scatter(
        times_transpose(grad_ups, gates_full).astype(bf16),
        "tensor",
        scatter_dimension=0,
        tiled=True,
    ).astype(f32)
    grad_gain_two = jnp.sum(grad_normed_two * unit_two, axis=0)
    grad_middle = cotangent.astype(f32) + norm_backward(
        grad_normed_two, unit_two, scale_two, gain_two
    )
    mid_full = lax.all_gather(grad_middle.astype(bf16), "tensor", axis=0, tiled=True)

    mid_full, hidden, grad_ups_late = lax.optimization_barrier((mid_full, hidden, grad_ups))
    ffn_grads = jnp.concatenate(
        [
            weight_grad(normed_two, grad_ups_late).astype(bf16),
            weight_grad(cot_full, hidden).astype(bf16),
            weight_grad(mid_full, mixed).astype(bf16),
        ],
        axis=1,
    )
    ffn_sums = lax.psum_scatter(ffn_grads, "dp", scatter_dimension=0, tiled=True).astype(f32)
    result = (
        middle
        + lax.psum_scatter(
            times_transpose(hidden, down_full).astype(bf16),
            "tensor",
            scatter_dimension=0,
            tiled=True,
        ).astype(f32)
    ).astype(bf16)

    grad_mixed = jnp.dot(mid_full, out_full, preferred_element_type=f32)
    grad_conv_all, grad_pgate, grad_rates, grad_gain_row = mixer_backward(
        conv_all, proj_gate, rates, gain_row, states, inverses, grad_mixed,
        heads, key_dim, value_dim,
    )
    grad_pconv, grad_conv_w = conv_pull(grad_conv_all)
    grad_beta, grad_alpha, grad_rate_part, grad_bias_part = rates_pull(grad_rates)
    grad_proj = jnp.concatenate(
        [
            grad_pconv.astype(bf16),
            grad_pgate.astype(bf16),
            pad_columns(
                jnp.concatenate([grad_beta.astype(bf16), grad_alpha.astype(bf16)], axis=1), LANES
            ),
        ],
        axis=1,
    )
    grad_normed_part = times_transpose(grad_proj, in_full)
    grad_normed_one = lax.psum_scatter(
        grad_normed_part.astype(bf16), "tensor", scatter_dimension=0, tiled=True
    ).astype(f32)
    grad_gain_one = jnp.sum(grad_normed_one * unit_one, axis=0)
    grad_rows = grad_middle + norm_backward(grad_normed_one, unit_one, scale_one, gain_one)

    def conv_grad(start, width, channels):
        part = grad_conv_w[start : start + width].reshape(heads, channels, taps)
        return jnp.swapaxes(part, 0, 1)

    conv_q_grad = conv_grad(0, qk_width, key_dim)
    conv_k_grad = conv_grad(qk_width, qk_width, key_dim)
    conv_v_grad = conv_grad(2 * qk_width, v_width, value_dim)
    head_gain_grad = grad_gain_row.reshape(heads, value_dim).T

    def grad_columns(values):
        shards = values.reshape(dp, -1)
        size = shards.shape[1]
        shards = jnp.pad(shards, ((0, 0), (0, round_up(size, shard_rows) - size)))
        return shards.reshape(model, -1)

    tail_cols = pad_columns(
        jnp.concatenate(
            [grad_columns(g) for g in (conv_q_grad, conv_k_grad, conv_v_grad, head_gain_grad)],
            axis=1,
        ),
        LANES,
    )
    mixer_grads = jnp.concatenate(
        [weight_grad(normed_one, grad_proj).astype(bf16), tail_cols.astype(bf16)], axis=1
    )
    mixer_sums = lax.psum_scatter(mixer_grads, "dp", scatter_dimension=0, tiled=True).astype(f32)

    head_total = heads * lax.axis_size("tensor")
    head_start = lax.axis_index("tensor") * heads

    def place_heads(local_grad):
        return lax.dynamic_update_slice(
            jnp.zeros((head_total,), f32), local_grad, (head_start,)
        )

    gain_parts = jnp.concatenate(
        [grad_gain_one, grad_gain_two, place_heads(grad_rate_part), place_heads(grad_bias_part)]
    )
    summed = lax.psum(gain_parts, ("dp", "tensor"))
    shard_start = lax.axis_index("dp") * shard_rows
    grad_gain_one_shard = lax.dynamic_slice_in_dim(summed, shard_start, shard_rows, 0)
    grad_gain_two_shard = lax.dynamic_slice_in_dim(summed, model + shard_start, shard_rows, 0)
    grad_rate = lax.dynamic_slice_in_dim(summed, 2 * model + head_start, heads, 0)
    grad_rate_bias = lax.dynamic_slice_in_dim(
        summed, 2 * model + head_total + head_start, heads, 0
    )

    def small_sum(index, at):
        shape, size = small_arrays[index].shape, small_arrays[index].size
        cols = mixer_sums[:, in_width + at : in_width + at + counts[index]]
        return cols.reshape(-1)[:size].reshape(shape)

    return (
        result,
        grad_rows,
        grad_gain_one_shard,
        mixer_sums[:, :qk_width],
        mixer_sums[:, qk_width : 2 * qk_width],
        mixer_sums[:, 2 * qk_width : conv_width],
        mixer_sums[:, conv_width:small_at],
        ffn_sums[:, 3 * ff :],
        mixer_sums[:, small_at : small_at + heads],
        mixer_sums[:, small_at + heads : small_at + 2 * heads],
        small_sum(2, 0),
        small_sum(3, counts[2]),
        small_sum(4, counts[2] + counts[3]),
        grad_rate,
        grad_rate_bias,
        small_sum(5, counts[2] + counts[3] + counts[4]),
        grad_gain_two_shard,
        ffn_sums[:, :hidden_width],
        ffn_sums[:, ff : ff + hidden_width],
        ffn_sums[:, 2 * ff : 2 * ff + hidden_width],
    )


def solution(mesh):
    placed = (
        P(("dp", "tensor"), None),
        P(("dp", "tensor"), None),
        P("dp"),
        P("dp", "tensor"),
        P("dp", "tensor"),
        P("dp", "tensor"),
        P("dp", "tensor"),
        P("dp", "tensor"),
        P("dp", "tensor"),
        P("dp", "tensor"),
        P("dp", "tensor", None),
        P("dp", "tensor", None),
        P("dp", "tensor", None),
        P("tensor"),
        P("tensor"),
        P("dp", "tensor"),
        P("dp"),
        P("dp", "tensor"),
        P("dp", "tensor"),
        P("dp", "tensor"),
    )
    return jax.shard_map(
        on_device,
        mesh=mesh,
        in_specs=placed,
        out_specs=(
            P(("dp", "tensor"), None),
            P(("dp", "tensor"), None),
            P("dp"),
            P("dp", "tensor"),
            P("dp", "tensor"),
            P("dp", "tensor"),
            P("dp", "tensor"),
            P("dp", "tensor"),
            P("dp", "tensor"),
            P("dp", "tensor"),
            P("dp", "tensor", None),
            P("dp", "tensor", None),
            P("dp", "tensor", None),
            P("tensor"),
            P("tensor"),
            P("dp", "tensor"),
            P("dp"),
            P("dp", "tensor"),
            P("dp", "tensor"),
            P("dp", "tensor"),
        ),
        check_vma=False,
    )
```

```python
import jax
import jax.numpy as jnp
from jax import lax
from jax.experimental import pallas as pl
from jax.experimental.pallas import tpu as pltpu
from jax.sharding import PartitionSpec as P

epsilon = 1e-06
CHUNK = 128
LANES = 128
contract_rows = (((0,), (0,)), ((), ()))
contract_cols = (((1,), (1,)), ((), ()))
contract_plain = (((1,), (0,)), ((), ()))
highest = lax.Precision.HIGHEST


def norm_forward(row_values):
    row_scale = lax.rsqrt(jnp.mean(row_values * row_values, axis=-1, keepdims=True) + epsilon)
    return (row_scale, row_values * row_scale)


def norm_backward(grad_normed, unit_values, row_scale, gain_values):
    grad_unit = grad_normed * gain_values
    return row_scale * (
        grad_unit - unit_values * jnp.mean(grad_unit * unit_values, axis=-1, keepdims=True)
    )


def weight_grad(left_in, right_in):
    return lax.dot_general(left_in, right_in, contract_rows, preferred_element_type=jnp.float32)


def times_transpose(left_in, right_in):
    return lax.dot_general(left_in, right_in, contract_cols, preferred_element_type=jnp.float32)


def exact_dot(left_in, right_in, dims=contract_plain):
    return lax.dot_general(
        left_in, right_in, dims, precision=highest, preferred_element_type=jnp.float32
    )


def silu(values):
    return values * lax.logistic(values)


def unit_length(values):
    return values * lax.rsqrt(jnp.sum(values * values, axis=-1, keepdims=True) + epsilon)


def triangle_masks(size):
    row = lax.broadcasted_iota(jnp.int32, (size, size), 0)
    col = lax.broadcasted_iota(jnp.int32, (size, size), 1)
    return row, col


def unit_lower_inverse(lower):
    size = lower.shape[0]
    row, col = triangle_masks(size)
    inverse = jnp.where(row == col, 1.0, 0.0)
    bit = 0
    while (1 << bit) < size:
        joined = ((row >> (bit + 1)) == (col >> (bit + 1))) & ((row >> bit) != (col >> bit))
        part = jnp.where(joined, lower, 0.0)
        if bit == 0:
            inverse = inverse - part
        else:
            inverse = inverse - exact_dot(inverse, exact_dot(part, inverse))
        bit += 1
    return inverse


@jax.custom_vjp
def known_inverse(lower, inverse):
    return inverse


def known_inverse_fwd(lower, inverse):
    return inverse, inverse


def known_inverse_bwd(inverse, grad):
    turned = inverse.T
    return -exact_dot(exact_dot(turned, grad), turned), jnp.zeros_like(inverse)


known_inverse.defvjp(known_inverse_fwd, known_inverse_bwd)


def mixer_chunk(conv_q, conv_k, conv_v, proj_gate, beta, gate, gain, state, inverter):
    size, key_dim = conv_q.shape
    row, col = triangle_masks(size)
    strict = row > col
    lower = row >= col
    query = unit_length(silu(conv_q)) * key_dim ** (-0.5)
    key = unit_length(silu(conv_k))
    value = silu(conv_v)
    wide = jnp.broadcast_to(gate, (size, size))
    decay_col = jnp.sum(jnp.where(lower, wide.T, 0.0), axis=1, keepdims=True)
    decay_row = jnp.sum(jnp.where(row <= col, wide, 0.0), axis=0, keepdims=True)
    decay_end = jnp.sum(gate, axis=0, keepdims=True)
    differ = jnp.where(strict, decay_col - decay_row, 0.0)
    decay = jnp.where(lower, jnp.exp(differ), 0.0)
    system = jnp.where(strict, exact_dot(key, key, contract_cols) * decay * beta, 0.0)
    inverse = inverter(system)
    grown = jnp.exp(decay_col)
    fresh = exact_dot(inverse, value * beta - exact_dot(key * (beta * grown), state))
    scores = exact_dot(query, key, contract_cols) * decay
    mixed = exact_dot(query * grown, state) + exact_dot(scores, fresh)
    new_state = jnp.exp(decay_end) * state + exact_dot(
        key * jnp.exp(decay_end - decay_col), fresh, contract_rows
    )
    scaled = mixed * lax.rsqrt(jnp.mean(mixed * mixed, axis=-1, keepdims=True) + epsilon) * gain
    return scaled * silu(proj_gate), new_state, inverse


def head_slices(head, heads, key_dim, value_dim):
    q_at = head * key_dim
    k_at = (heads + head) * key_dim
    v_at = 2 * heads * key_dim + head * value_dim
    return (
        slice(q_at, q_at + key_dim),
        slice(k_at, k_at + key_dim),
        slice(v_at, v_at + value_dim),
        slice(head * value_dim, (head + 1) * value_dim),
    )


def mixer_forward_kernel(
    heads, key_dim, value_dim, conv_ref, pgate_ref, rates_ref, gain_ref,
    gated_ref, states_ref, inverses_ref, state_ref,
):
    @pl.when(pl.program_id(0) == 0)
    def _():
        state_ref[...] = jnp.zeros_like(state_ref)

    for head in range(heads):
        at_q, at_k, at_v, at_g = head_slices(head, heads, key_dim, value_dim)
        state = state_ref[head]
        gated, new_state, inverse = mixer_chunk(
            conv_ref[:, at_q],
            conv_ref[:, at_k],
            conv_ref[:, at_v],
            pgate_ref[:, at_g],
            rates_ref[:, head : head + 1],
            rates_ref[:, heads + head : heads + head + 1],
            gain_ref[:, at_g],
            state,
            unit_lower_inverse,
        )
        gated_ref[:, at_g] = gated.astype(gated_ref.dtype)
        states_ref[0, head] = state
        inverses_ref[0, head] = inverse
        state_ref[head] = new_state


def mixer_backward_kernel(
    heads, key_dim, value_dim, conv_ref, pgate_ref, rates_ref, gain_ref, states_ref,
    inverses_ref, grad_ref, gconv_ref, gpgate_ref, grates_ref, ggain_ref, gstate_ref,
):
    @pl.when(pl.program_id(0) == 0)
    def _():
        gstate_ref[...] = jnp.zeros_like(gstate_ref)
        ggain_ref[...] = jnp.zeros_like(ggain_ref)

    lane = lax.broadcasted_iota(jnp.int32, grates_ref.shape, 1)
    rates_grad = jnp.zeros(grates_ref.shape, jnp.float32)
    for head in range(heads):
        at_q, at_k, at_v, at_g = head_slices(head, heads, key_dim, value_dim)
        inverse = inverses_ref[0, head]

        def run(*operands):
            gated, new_state, _ = mixer_chunk(
                *operands, lambda system: known_inverse(system, inverse)
            )
            return gated, new_state

        _, pull = jax.vjp(
            run,
            conv_ref[:, at_q],
            conv_ref[:, at_k],
            conv_ref[:, at_v],
            pgate_ref[:, at_g],
            rates_ref[:, head : head + 1],
            rates_ref[:, heads + head : heads + head + 1],
            gain_ref[:, at_g],
            states_ref[0, head],
        )
        pulled = pull((grad_ref[:, at_g], gstate_ref[head]))
        gconv_ref[:, at_q] = pulled[0]
        gconv_ref[:, at_k] = pulled[1]
        gconv_ref[:, at_v] = pulled[2]
        gpgate_ref[:, at_g] = pulled[3]
        rates_grad = jnp.where(lane == head, pulled[4], rates_grad)
        rates_grad = jnp.where(lane == heads + head, pulled[5], rates_grad)
        ggain_ref[:, at_g] += pulled[6]
        gstate_ref[head] = pulled[7]
    grates_ref[...] = rates_grad


def row_block(width, order):
    return pl.BlockSpec((CHUNK, width), lambda step: (order(step), 0))


def mixer_forward(conv_all, proj_gate, rates, gain_row, heads, key_dim, value_dim):
    rows, conv_width = conv_all.shape
    steps = rows // CHUNK
    forward = lambda step: step
    width = heads * value_dim
    return pl.pallas_call(
        lambda *refs: mixer_forward_kernel(heads, key_dim, value_dim, *refs),
        name="mixer_forward",
        grid=(steps,),
        in_specs=[
            row_block(conv_width, forward),
            row_block(width, forward),
            row_block(rates.shape[1], forward),
            pl.BlockSpec((1, width), lambda step: (0, 0)),
        ],
        out_specs=[
            row_block(width, forward),
            pl.BlockSpec((1, heads, key_dim, value_dim), lambda step: (step, 0, 0, 0)),
            pl.BlockSpec((1, heads, CHUNK, CHUNK), lambda step: (step, 0, 0, 0)),
        ],
        out_shape=[
            jax.ShapeDtypeStruct((rows, width), jnp.bfloat16),
            jax.ShapeDtypeStruct((steps, heads, key_dim, value_dim), jnp.float32),
            jax.ShapeDtypeStruct((steps, heads, CHUNK, CHUNK), jnp.float32),
        ],
        scratch_shapes=[pltpu.VMEM((heads, key_dim, value_dim), jnp.float32)],
        cost_estimate=pl.CostEstimate(
            flops=30_000_000_000, bytes_accessed=8_000_000, transcendentals=1_000_000
        ),
    )(conv_all, proj_gate, rates, gain_row)


def mixer_backward(
    conv_all, proj_gate, rates, gain_row, states, inverses, grad_gated, heads, key_dim, value_dim
):
    rows, conv_width = conv_all.shape
    steps = rows // CHUNK
    back = lambda step: steps - 1 - step
    width = heads * value_dim
    return pl.pallas_call(
        lambda *refs: mixer_backward_kernel(heads, key_dim, value_dim, *refs),
        name="mixer_backward",
        grid=(steps,),
        in_specs=[
            row_block(conv_width, back),
            row_block(width, back),
            row_block(rates.shape[1], back),
            pl.BlockSpec((1, width), lambda step: (0, 0)),
            pl.BlockSpec((1, heads, key_dim, value_dim), lambda step: (back(step), 0, 0, 0)),
            pl.BlockSpec((1, heads, CHUNK, CHUNK), lambda step: (back(step), 0, 0, 0)),
            row_block(width, back),
        ],
        out_specs=[
            row_block(conv_width, back),
            row_block(width, back),
            row_block(rates.shape[1], back),
            pl.BlockSpec((1, width), lambda step: (0, 0)),
        ],
        out_shape=[
            jax.ShapeDtypeStruct((rows, conv_width), jnp.float32),
            jax.ShapeDtypeStruct((rows, width), jnp.float32),
            jax.ShapeDtypeStruct(rates.shape, jnp.float32),
            jax.ShapeDtypeStruct((1, width), jnp.float32),
        ],
        scratch_shapes=[pltpu.VMEM((heads, key_dim, value_dim), jnp.float32)],
        cost_estimate=pl.CostEstimate(
            flops=30_000_000_000, bytes_accessed=12_000_000, transcendentals=2_000_000
        ),
    )(conv_all, proj_gate, rates, gain_row, states, inverses, grad_gated)


def exchange_kernel(axis, ranks, scatter, block_ref, got_ref, send_sems, recv_sems):
    me = lax.axis_index(axis)
    barrier = pltpu.get_barrier_semaphore()
    for step in range(1, ranks):
        pl.semaphore_signal(
            barrier,
            inc=1,
            device_id={axis: lax.rem(me + step, ranks)},
            device_id_type=pl.DeviceIdType.MESH,
        )
    pl.semaphore_wait(barrier, ranks - 1)
    copies = []
    for step in range(1, ranks):
        peer = lax.rem(me + step, ranks)
        copy = pltpu.make_async_remote_copy(
            src_ref=block_ref.at[peer] if scatter else block_ref.at[0],
            dst_ref=got_ref.at[me],
            send_sem=send_sems.at[step - 1],
            recv_sem=recv_sems.at[step - 1],
            device_id={axis: peer},
            device_id_type=pl.DeviceIdType.MESH,
        )
        copy.start()
        copies.append(copy)
    got_ref[me] = block_ref[me] if scatter else block_ref[0]
    for copy in copies:
        copy.wait()


def exchange(blocks, axis, number, scatter):
    ranks = lax.axis_size(axis)
    return pl.pallas_call(
        lambda *refs: exchange_kernel(axis, ranks, scatter, *refs),
        name="exchange",
        in_specs=[pl.BlockSpec(memory_space=pltpu.VMEM)],
        out_specs=pl.BlockSpec(memory_space=pltpu.VMEM),
        out_shape=jax.ShapeDtypeStruct((ranks,) + blocks.shape[1:], blocks.dtype),
        scratch_shapes=[
            pltpu.SemaphoreType.DMA((ranks - 1,)),
            pltpu.SemaphoreType.DMA((ranks - 1,)),
        ],
        compiler_params=pltpu.CompilerParams(collective_id=number, has_side_effects=True),
        cost_estimate=pl.CostEstimate(
            flops=10_000_000_000, bytes_accessed=blocks.size * 4, transcendentals=0
        ),
    )(blocks)


def gather_rows(block, axis, number):
    got = exchange(block[None], axis, number, False)
    return got.reshape(-1, block.shape[1])


def scatter_sum(partial, axis, number):
    ranks = lax.axis_size(axis)
    got = exchange(partial.reshape(ranks, -1, partial.shape[1]), axis, number, True)
    return jnp.sum(got.astype(jnp.float32), axis=0)


def short_conv(inputs, weights):
    tap_count = weights.shape[1]
    row_count = inputs.shape[0]
    padded = jnp.pad(inputs, ((tap_count - 1, 0), (0, 0)))
    result = jnp.zeros_like(inputs)
    for offset in range(tap_count):
        result = result + padded[offset : offset + row_count] * weights[:, offset]
    return result


def channel_weights(conv_weights):
    key_dim, head_count, tap_count = conv_weights.shape
    return jnp.swapaxes(conv_weights, 0, 1).reshape(head_count * key_dim, tap_count)


def pad_columns(matrix_in, width):
    return jnp.pad(matrix_in, ((0, 0), (0, width - matrix_in.shape[1])))


def round_up(size, step):
    return -(-size // step) * step


def as_columns(values, rows):
    flat = values.reshape(-1)
    return jnp.pad(flat, (0, round_up(flat.shape[0], rows) - flat.shape[0])).reshape(rows, -1)


def rate_terms(proj_beta, proj_alpha, log_rate, rate_bias):
    log_gates = -jnp.exp(log_rate) * jax.nn.softplus(proj_alpha + rate_bias)
    return jnp.concatenate([jax.nn.sigmoid(proj_beta), log_gates], axis=1)


def on_device(
    tokens, cotangent, norm1_gain, w_query, w_key, w_value, w_gate_out, w_out, w_beta, w_alpha,
    conv_query, conv_key, conv_value, a_log, dt_bias, head_gain, norm2_gain, w_up_gate, w_up,
    w_down,
):
    bf16, f32 = jnp.bfloat16, jnp.float32
    shard_rows, model = w_query.shape[0], tokens.shape[1]
    dp = model // shard_rows
    heads = a_log.shape[0]
    key_dim, value_dim = w_query.shape[1] // heads, w_value.shape[1] // heads
    taps = conv_query.shape[2]
    qk_width, v_width = heads * key_dim, heads * value_dim
    conv_width = 2 * qk_width + v_width
    hidden_width = w_up.shape[1]
    ff = round_up(hidden_width, 256)

    small_arrays = (norm1_gain, norm2_gain, conv_query, conv_key, conv_value, head_gain)
    small_cols = [as_columns(values, shard_rows) for values in small_arrays]
    counts = [cols.shape[1] for cols in small_cols]
    small = pad_columns(jnp.concatenate([w_beta, w_alpha] + small_cols, axis=1), LANES)
    mixer_pack = jnp.concatenate([w_query, w_key, w_value, w_gate_out, small, w_out], axis=1)
    in_width = conv_width + v_width + LANES
    rows_pack = jnp.concatenate([tokens, cotangent], axis=1)
    rows_full = gather_rows(rows_pack, "tensor", 1)
    mixer_full = lax.all_gather(mixer_pack, "dp", axis=0, tiled=True)
    ffn_pack = jnp.concatenate([pad_columns(w, ff) for w in (w_up_gate, w_up, w_down)], axis=1)
    mixer_full, ffn_pack = lax.optimization_barrier((mixer_full, ffn_pack))
    ffn_full = lax.all_gather(ffn_pack, "dp", axis=0, tiled=True)

    in_full = mixer_full[:, :in_width]
    out_full = mixer_full[:, in_width:]
    starts = [2 * heads]
    for count in counts:
        starts.append(starts[-1] + count)
    small_at = conv_width + v_width

    def unpacked(index):
        cols = mixer_full[:, small_at + starts[index] : small_at + starts[index + 1]]
        shape = small_arrays[index].shape
        size = small_arrays[index].size
        shards = cols.reshape(dp, -1)[:, :size]
        return shards.reshape((dp * shape[0],) + shape[1:]).astype(f32)

    gain_one, gain_two = unpacked(0), unpacked(1)
    conv_weights = jnp.concatenate([channel_weights(unpacked(i)) for i in (2, 3, 4)], axis=0)
    gain_row = unpacked(5).T.reshape(1, v_width)

    tokens_full = rows_full[:, :model].astype(f32)
    cot_full = rows_full[:, model:]
    _, unit_full = norm_forward(tokens_full)
    normed_one = (unit_full * gain_one).astype(bf16)
    projected = jnp.dot(normed_one, in_full, preferred_element_type=f32)
    proj_conv = projected[:, :conv_width]
    proj_gate = projected[:, conv_width:small_at]
    proj_beta = projected[:, small_at : small_at + heads]
    proj_alpha = projected[:, small_at + heads : small_at + 2 * heads]
    conv_all, conv_pull = jax.vjp(short_conv, proj_conv, conv_weights)
    rates, rates_pull = jax.vjp(
        rate_terms, proj_beta, proj_alpha, a_log.astype(f32), dt_bias.astype(f32)
    )
    mixed, states, inverses = mixer_forward(
        conv_all, proj_gate, rates, gain_row, heads, key_dim, value_dim
    )
    row_values = tokens.astype(f32)
    scale_one, unit_one = norm_forward(row_values)
    middle = row_values + scatter_sum(
        times_transpose(mixed, out_full).astype(bf16), "tensor", 2
    )
    gates_full, down_full = ffn_full[:, : 2 * ff], ffn_full[:, 2 * ff :]
    grad_hidden = jnp.dot(cot_full, down_full, preferred_element_type=f32)
    scale_two, unit_two = norm_forward(middle)
    normed_two = gather_rows((unit_two * gain_two).astype(bf16), "tensor", 3)
    ups = jnp.dot(normed_two, gates_full, preferred_element_type=f32)
    up_gate, up_lin = ups[:, :ff], ups[:, ff:]
    gate_sigmoid = jax.nn.sigmoid(up_gate)
    hidden = (up_gate * gate_sigmoid * up_lin).astype(bf16)
    grad_gate = (
        grad_hidden * up_lin * gate_sigmoid * (1.0 + up_gate * (1.0 - gate_sigmoid))
    ).astype(bf16)
    grad_lin = (grad_hidden * up_gate * gate_sigmoid).astype(bf16)
    grad_ups = jnp.concatenate([grad_gate, grad_lin], axis=1)
    grad_normed_two = scatter_sum(
        times_transpose(grad_ups, gates_full).astype(bf16), "tensor", 4
    )
    ffn_grads = jnp.concatenate(
        [
            weight_grad(normed_two, grad_ups).astype(bf16),
            weight_grad(cot_full, hidden).astype(bf16),
        ],
        axis=1,
    )
    grad_normed_two, ffn_grads = lax.optimization_barrier((grad_normed_two, ffn_grads))
    ffn_sums = lax.psum_scatter(ffn_grads, "dp", scatter_dimension=0, tiled=True)
    grad_gain_two = jnp.sum(grad_normed_two * unit_two, axis=0)
    grad_middle = cotangent.astype(f32) + norm_backward(
        grad_normed_two, unit_two, scale_two, gain_two
    )
    mid_full = gather_rows(grad_middle.astype(bf16), "tensor", 5)
    out_grads = weight_grad(mid_full, mixed).astype(bf16)
    out_grads, mid_full = lax.optimization_barrier((out_grads, mid_full))
    out_grads, ffn_sums = lax.optimization_barrier((out_grads, ffn_sums))
    out_sums = lax.psum_scatter(out_grads, "dp", scatter_dimension=0, tiled=True)
    result = (
        middle + scatter_sum(times_transpose(hidden, down_full).astype(bf16), "tensor", 6)
    ).astype(bf16)

    grad_mixed = jnp.dot(mid_full, out_full, preferred_element_type=f32)
    grad_conv_all, grad_pgate, grad_rates, grad_gain_row = mixer_backward(
        conv_all, proj_gate, rates, gain_row, states, inverses, grad_mixed,
        heads, key_dim, value_dim,
    )
    grad_pconv, grad_conv_w = conv_pull(grad_conv_all)
    grad_beta, grad_alpha, grad_rate_part, grad_bias_part = rates_pull(grad_rates)
    grad_proj = jnp.concatenate(
        [
            grad_pconv.astype(bf16),
            grad_pgate.astype(bf16),
            pad_columns(
                jnp.concatenate([grad_beta.astype(bf16), grad_alpha.astype(bf16)], axis=1), LANES
            ),
        ],
        axis=1,
    )
    grad_normed_part = times_transpose(grad_proj, in_full)
    ranks = lax.axis_size("tensor")
    gain_lines = jnp.stack([jnp.sum(grad_normed_part * unit_full, axis=0), grad_gain_two])
    gain_lines = jnp.pad(gain_lines, ((0, 14), (0, 0))).astype(bf16)
    sent = jnp.concatenate(
        [
            grad_normed_part.astype(bf16).reshape(ranks, -1, model),
            jnp.broadcast_to(gain_lines, (ranks,) + gain_lines.shape),
        ],
        axis=1,
    )
    received = scatter_sum(sent.reshape(-1, model), "tensor", 7)
    own_rows = tokens.shape[0]
    grad_normed_one = received[:own_rows]
    gain_columns = received[own_rows : own_rows + 2].T
    grad_rows = grad_middle + norm_backward(grad_normed_one, unit_one, scale_one, gain_one)

    def conv_grad(start, width, channels):
        part = grad_conv_w[start : start + width].reshape(heads, channels, taps)
        return jnp.swapaxes(part, 0, 1)

    conv_q_grad = conv_grad(0, qk_width, key_dim)
    conv_k_grad = conv_grad(qk_width, qk_width, key_dim)
    conv_v_grad = conv_grad(2 * qk_width, v_width, value_dim)
    head_gain_grad = grad_gain_row.reshape(heads, value_dim).T

    def grad_columns(values):
        shards = values.reshape(dp, -1)
        size = shards.shape[1]
        shards = jnp.pad(shards, ((0, 0), (0, round_up(size, shard_rows) - size)))
        return shards.reshape(model, -1)

    rate_line = jnp.concatenate([grad_rate_part, grad_bias_part])
    rate_tile = jnp.pad(rate_line[None], ((0, 7), (0, LANES - 2 * heads)))
    rate_sums = jnp.sum(exchange(rate_tile[None], "dp", 8, False), axis=0)[0]
    tail_cols = pad_columns(
        jnp.concatenate(
            [grad_columns(g) for g in (conv_q_grad, conv_k_grad, conv_v_grad, head_gain_grad)]
            + [gain_columns],
            axis=1,
        ),
        LANES,
    )
    mixer_grads = jnp.concatenate(
        [weight_grad(normed_one, grad_proj).astype(bf16), tail_cols.astype(bf16)], axis=1
    )
    mixer_grads, out_sums = lax.optimization_barrier((mixer_grads, out_sums))
    mixer_sums = lax.psum_scatter(mixer_grads, "dp", scatter_dimension=0, tiled=True).astype(f32)
    out_sums, ffn_sums = out_sums.astype(f32), ffn_sums.astype(f32)
    small_end = in_width + sum(counts[2:])
    grad_rate = rate_sums[:heads]
    grad_rate_bias = rate_sums[heads : 2 * heads]

    def small_sum(index, at):
        shape, size = small_arrays[index].shape, small_arrays[index].size
        cols = mixer_sums[:, in_width + at : in_width + at + counts[index]]
        return cols.reshape(-1)[:size].reshape(shape)

    return (
        result,
        grad_rows,
        mixer_sums[:, small_end],
        mixer_sums[:, :qk_width],
        mixer_sums[:, qk_width : 2 * qk_width],
        mixer_sums[:, 2 * qk_width : conv_width],
        mixer_sums[:, conv_width:small_at],
        out_sums,
        mixer_sums[:, small_at : small_at + heads],
        mixer_sums[:, small_at + heads : small_at + 2 * heads],
        small_sum(2, 0),
        small_sum(3, counts[2]),
        small_sum(4, counts[2] + counts[3]),
        grad_rate,
        grad_rate_bias,
        small_sum(5, counts[2] + counts[3] + counts[4]),
        mixer_sums[:, small_end + 1],
        ffn_sums[:, :hidden_width],
        ffn_sums[:, ff : ff + hidden_width],
        ffn_sums[:, 2 * ff : 2 * ff + hidden_width],
    )


def solution(mesh):
    placed = (
        P(("dp", "tensor"), None),
        P(("dp", "tensor"), None),
        P("dp"),
        P("dp", "tensor"),
        P("dp", "tensor"),
        P("dp", "tensor"),
        P("dp", "tensor"),
        P("dp", "tensor"),
        P("dp", "tensor"),
        P("dp", "tensor"),
        P("dp", "tensor", None),
        P("dp", "tensor", None),
        P("dp", "tensor", None),
        P("tensor"),
        P("tensor"),
        P("dp", "tensor"),
        P("dp"),
        P("dp", "tensor"),
        P("dp", "tensor"),
        P("dp", "tensor"),
    )
    return jax.shard_map(
        on_device,
        mesh=mesh,
        in_specs=placed,
        out_specs=(
            P(("dp", "tensor"), None),
            P(("dp", "tensor"), None),
            P("dp"),
            P("dp", "tensor"),
            P("dp", "tensor"),
            P("dp", "tensor"),
            P("dp", "tensor"),
            P("dp", "tensor"),
            P("dp", "tensor"),
            P("dp", "tensor"),
            P("dp", "tensor", None),
            P("dp", "tensor", None),
            P("dp", "tensor", None),
            P("tensor"),
            P("tensor"),
            P("dp", "tensor"),
            P("dp"),
            P("dp", "tensor"),
            P("dp", "tensor"),
            P("dp", "tensor"),
        ),
        check_vma=False,
    )
```
